32 devices in a mesh: rep: 16 (over z, y, x), tp: 2 (over core).
Axes of the slice: x: 2, y: 2, z: 4, core: 2. Of those that a mesh axis runs over, the one named last changes fastest.
Arguments:
- tokens: bfloat16 [2048, 4096], P('rep'), may hold values from -6 to 6
- targets: bfloat16 [2048, 4096], P('rep'), may hold values from -6 to 6
- frozen_in_matrix: bfloat16 [4096, 8192], P('rep', 'tp'), may hold values from -6 to 6
- base_out: bfloat16 [8192, 4096], P('tp', 'rep'), may hold values from -6 to 6
- factor_down: bfloat16 [16, 16, 4096], P('rep'), may hold values from -6 to 6
- factor_up: bfloat16 [16, 16, 8192], P('rep', None, 'tp'), may hold values from -0.75 to 0.75
Outputs:
- merged: float32 [4096, 8192], P('rep', 'tp')
- new_down: float32 [16, 16, 4096], P('rep')
- new_up: float32 [16, 16, 8192], P('rep', None, 'tp')
The draws below stay inside these ranges and needn't reach their ends.
All inputs are finite; a program needn't handle non-finite values.
Results may differ from the reference program's by a relative error of at most 0.014.
The reference program's roundings to bfloat16 on the way count: a program that leaves them out, or rounds other values in their place, can miss the bound.
Values may be sent and summed in bfloat16 or wider, within the bound.
A program may use at most 128 MiB of HBM per device.

```python
import jax
import jax.numpy as jnp
from jax import lax

MODEL_WIDTH = 4096
FF = 8192
RANK = 16
TOK_DEV = 128
REPLICA_COUNT = 16
TOKENS = 2048


def shard_levels(rng, shape, split, least, top_value):
    level, own = 1.0, jax.random.fold_in(rng, 6)
    for position, parts in split:
        draws = jnp.exp(jax.random.uniform(jax.random.fold_in(own, position), (parts,), jnp.float32, least / len(split), top_value / len(split)))
        level = level * jnp.repeat(draws, shape[position] // parts).reshape([-1 if axis == position else 1 for axis in range(len(shape))])
    return level


def gaussian(key, shape, scale, reach, shards=(), dtype=jnp.bfloat16):
    result = jax.random.normal(key, shape, jnp.float32) * scale
    if len(shards) > 0:
        result = shard_levels(key, shape, shards, -0.22, 0.18) * result
    return jnp.clip(result, min=-reach, max=reach).astype(dtype)


def setup_inputs(seed: int = 0) -> dict:
    seeds = jax.random.split(jax.random.key(seed), 7)
    tokens = gaussian(seeds[0], (TOKENS, MODEL_WIDTH), 1.0, 6.0, ((0, 16),))
    targets = gaussian(seeds[1], (TOKENS, MODEL_WIDTH), 1.0, 6.0, ((0, 16),))
    frozen_in_matrix = gaussian(seeds[2], (MODEL_WIDTH, FF), 1.0, 6.0, ((0, 16), (1, 2)))
    base_out = gaussian(seeds[3], (FF, MODEL_WIDTH), 1.0, 6.0, ((0, 2), (1, 16)))
    factor_down = gaussian(seeds[4], (REPLICA_COUNT, RANK, MODEL_WIDTH), 1.0, 6.0, ((0, 16),))
    factor_up = gaussian(seeds[5], (REPLICA_COUNT, RANK, FF), 0.125, 0.75, ((0, 16), (2, 2)))
    return {"tokens": tokens, "targets": targets, "frozen_in_matrix": frozen_in_matrix, "base_out": base_out, "factor_down": factor_down, "factor_up": factor_up}


adapter_scale = 2.0
rate_down = 25.0
rate_up = 0.75


def replica_step(inputs, frozen_in_matrix, base_out):
    tokens, targets, factor_a, second_factor = inputs
    projection_result = jnp.dot(tokens, factor_a.T, preferred_element_type=jnp.float32).astype(jnp.bfloat16)
    preact = (jnp.dot(tokens, frozen_in_matrix, preferred_element_type=jnp.float32)
              + adapter_scale * jnp.dot(projection_result, second_factor, preferred_element_type=jnp.float32)) * (MODEL_WIDTH ** -0.5)
    hidden = jnp.maximum(preact, 0.0).astype(jnp.bfloat16)
    output = jnp.dot(hidden, base_out, preferred_element_type=jnp.float32) * (FF ** -0.5)
    out_grad = ((output - targets.astype(jnp.float32)) / TOK_DEV).astype(jnp.bfloat16)
    hid_full = jnp.dot(out_grad, base_out.T, preferred_element_type=jnp.float32) * (FF ** -0.5)
    hidden_gradient = jnp.where(preact > 0, hid_full, 0.0).astype(jnp.bfloat16)
    up_gradient = (adapter_scale * MODEL_WIDTH ** -0.5) * jnp.dot(projection_result.T, hidden_gradient, preferred_element_type=jnp.float32)
    backward_parts = jnp.dot(hidden_gradient, second_factor.T, preferred_element_type=jnp.float32)
    down_gradient = (adapter_scale * MODEL_WIDTH ** -0.5) * jnp.dot(backward_parts.T, tokens.astype(jnp.float32), precision=lax.Precision.HIGHEST)
    new_a = factor_a.astype(jnp.float32) - rate_down * down_gradient
    new_b = second_factor.astype(jnp.float32) - rate_up * up_gradient
    return new_a, new_b


def reference(tokens, targets, frozen_in_matrix, base_out, factor_down, factor_up):
    tok_blocks = tokens.reshape(REPLICA_COUNT, TOK_DEV, MODEL_WIDTH)
    tgt_blocks = targets.reshape(REPLICA_COUNT, TOK_DEV, MODEL_WIDTH)
    new_down, new_up = lax.map(lambda inputs: replica_step(inputs, frozen_in_matrix, base_out),
                               (tok_blocks, tgt_blocks, factor_down, factor_up))
    down_transport = new_down.astype(jnp.bfloat16).reshape(REPLICA_COUNT * RANK, MODEL_WIDTH)
    up_transport = new_up.astype(jnp.bfloat16).reshape(REPLICA_COUNT * RANK, FF)
    merged = frozen_in_matrix.astype(jnp.float32) + (adapter_scale / REPLICA_COUNT) * jnp.dot(down_transport.T, up_transport, preferred_element_type=jnp.float32)
    return merged, new_down, new_up
```

```python
import jax
import jax.numpy as jnp
from jax import lax
from jax.sharding import Mesh
from jax.sharding import PartitionSpec as P

BF16, F32 = jnp.bfloat16, jnp.float32
adapter_scale = 2.0
rate_down = 25.0
rate_up = 0.75
REP = ("z", "s")


def spread_weights(frozen, base_out):
    first = lax.all_to_all(frozen, "z", split_axis=1, concat_axis=0, tiled=True)
    first = lax.all_gather(first, "s", axis=0, tiled=True)
    second = lax.all_to_all(base_out, "z", split_axis=0, concat_axis=1, tiled=True)
    second = lax.all_gather(second, "s", axis=1, tiled=True)
    return first, second


def shards(tokens, targets, frozen, base_out, factor_down, factor_up):
    z_count, s_count, tp_count = (lax.axis_size(n) for n in ("z", "s", "tp"))
    rep_count = z_count * s_count
    tok, width = tokens.shape
    ff = base_out.shape[0] * tp_count
    rank = factor_down.shape[1]
    a, b = factor_down[0], factor_up[0]
    step_scale = adapter_scale * width ** (-0.5)

    def permuted(x):
        blocks = x.reshape(x.shape[0], z_count, s_count, width // rep_count)
        return blocks.transpose(0, 2, 1, 3).reshape(x.shape)

    first, second = spread_weights(frozen, base_out)
    group_tokens = lax.all_gather(permuted(tokens), "z", axis=0, tiled=True)
    projected = jnp.einsum("td,rd->tr", tokens, a, preferred_element_type=F32).astype(BF16)
    group_proj = lax.all_gather(projected, "z", axis=0, tiled=False)
    group_b = lax.all_to_all(b, "z", split_axis=1, concat_axis=0, tiled=True)
    units = group_b.shape[1]
    group_b = group_b.reshape(z_count, rank, units)

    lead = jnp.dot(group_tokens, first, preferred_element_type=F32)
    low = jnp.einsum("gtr,grf->gtf", group_proj, group_b, preferred_element_type=F32)
    preact = (lead + adapter_scale * low.reshape(lead.shape)) * width ** (-0.5)
    hidden = jnp.maximum(preact, 0.0).astype(BF16)
    part = jnp.dot(hidden, second, preferred_element_type=F32) * ff ** (-0.5)
    output = lax.psum_scatter(part.astype(BF16), ("z", "tp"), scatter_dimension=0, tiled=True)
    own = tok // tp_count
    wanted = lax.dynamic_slice_in_dim(targets, lax.axis_index("tp") * own, own, 0)
    out_grad = ((output.astype(F32) - permuted(wanted).astype(F32)) / tok).astype(BF16)
    group_grad = lax.all_gather(out_grad, ("z", "tp"), axis=0, tiled=True)
    hid_full = jnp.einsum("td,fd->tf", group_grad, second, preferred_element_type=F32)
    hid_grad = jnp.where(preact > 0, hid_full * ff ** (-0.5), 0.0).astype(BF16)
    hid_grad = hid_grad.reshape(z_count, tok, units)

    up_grad = step_scale * jnp.einsum("gtr,gtf->grf", group_proj, hid_grad, preferred_element_type=F32)
    up_grad = lax.all_to_all(up_grad, "z", split_axis=0, concat_axis=2, tiled=True)[0]
    back = jnp.einsum("grf,gtf->grt", group_b, hid_grad, preferred_element_type=F32)
    back = lax.dynamic_index_in_dim(lax.psum(back, ("z", "tp")), lax.axis_index("z"), 0, keepdims=False)
    down_grad = step_scale * jnp.dot(back, tokens.astype(F32), precision=lax.Precision.HIGHEST)

    new_a = a.astype(F32) - rate_down * down_grad
    new_b = b.astype(F32) - rate_up * up_grad
    ups = lax.all_gather(new_b.astype(BF16), REP, axis=0, tiled=True)
    downs = lax.all_to_all(new_a.astype(BF16)[None], REP, split_axis=2, concat_axis=0, tiled=True)
    downs = downs.reshape(rep_count * rank, frozen.shape[0])
    delta = jnp.einsum("kd,kf->df", downs, ups, preferred_element_type=F32)
    merged = frozen.astype(F32) + adapter_scale / rep_count * delta
    return merged, new_a[None], new_b[None]


def solution(mesh):
    reps, tps = mesh.shape["rep"], mesh.shape["tp"]
    s_count = 1 << ((reps.bit_length() - 1) // 2)
    cut = Mesh(mesh.devices.reshape(reps // s_count, s_count, tps), ("z", "s", "tp"))
    in_specs = (
        P(REP, None),
        P(REP, None),
        P(REP, "tp"),
        P("tp", REP),
        P(REP, None, None),
        P(REP, None, "tp"),
    )
    out_specs = (P(REP, "tp"), P(REP, None, None), P(REP, None, "tp"))
    return jax.shard_map(shards, mesh=cut, in_specs=in_specs, out_specs=out_specs, check_vma=False)
```

```python
import jax
import jax.numpy as jnp
from jax import lax
from jax.experimental import pallas as pl
from jax.experimental.pallas import tpu as pltpu
from jax.sharding import Mesh
from jax.sharding import PartitionSpec as P

BF16, F32 = jnp.bfloat16, jnp.float32
adapter_scale = 2.0
rate_down = 25.0
rate_up = 0.75
REP = ("z", "s")
MESH = pl.DeviceIdType.MESH


def spread_kernel(frozen, base_out, tokens, first, second, pooled, rows_buf, cols_buf, tok_buf,
                  hop_send, hop_recv, side_send, side_recv, tok_send, tok_recv, part_send, part_recv, own_sem):
    z_count, tp_count = lax.axis_size("z"), lax.axis_size("tp")
    z, s, t = (lax.axis_index(n) for n in ("z", "s", "tp"))
    across = s + 1 - 2 * (s % 2)
    along = s + 2 - 4 * ((s // 2) % 2)
    rows, units = rows_buf.shape
    tok = tokens.shape[0]
    part = tok // tp_count

    def source(m, owner):
        at = pl.ds(pl.multiple_of(owner * units, units), units)
        return base_out.at[at, :] if m else frozen.at[:, at]

    def slot(m, seat, owner):
        at = pl.ds(pl.multiple_of((seat * z_count + owner) * rows, rows), rows)
        return second.at[:, at] if m else first.at[at, :]

    def remote(src, dst, send, recv, **where):
        return pltpu.make_async_remote_copy(
            src_ref=src, dst_ref=dst, send_sem=send, recv_sem=recv, device_id=where, device_id_type=MESH
        )

    barrier = pltpu.get_barrier_semaphore()
    peers = [{"z": (z + d) % z_count} for d in range(1, z_count)]
    peers += [{"tp": (t + d) % tp_count} for d in range(1, tp_count)]
    peers += [{"s": across}, {"s": along}]
    for peer in peers:
        pl.semaphore_signal(barrier, inc=1, device_id=peer, device_id_type=MESH)
    pl.semaphore_wait(barrier, len(peers))

    def part_of(seat, piece):
        return pooled.at[pl.ds(pl.multiple_of(seat * tok + piece * part, part), part), :]

    hops, parts = {}, {}
    for d in range(1, z_count):
        to = (z + d) % z_count
        for m in range(2):
            hops[m, d] = remote(source(m, to), slot(m, s, z), hop_send.at[m, d], hop_recv.at[m, d], z=to)
            hops[m, d].start()
        mine = tokens.at[pl.ds(pl.multiple_of(t * part, part), part), :]
        parts[d] = remote(mine, part_of(z, t), part_send.at[d], part_recv.at[d], z=to)
        parts[d].start()

    sides = {}

    def side(m, d, kind, seat, src, **where):
        owner = (z - d + z_count) % z_count
        copy = remote(src, slot(m, seat, owner), side_send.at[m, d, kind], side_recv.at[m, d, kind], **where)
        sides[m, d, kind] = copy
        copy.start()

    def share(d):
        owner = (z - d + z_count) % z_count
        for m in range(2):
            if d:
                hops[m, d].wait_recv()
            src = slot(m, s, owner) if d else source(m, z)
            side(m, d, 0, s, src, s=across)
            side(m, d, 1, s, src, s=along)

    def corner(d):
        owner = (z - d + z_count) % z_count
        for m in range(2):
            sides[m, d, d % 2].wait_recv()
            if d % 2:
                side(m, d, 2, along, slot(m, along, owner), s=across)
            else:
                side(m, d, 2, across, slot(m, across, owner), s=along)

    share(0)
    loads = [
        pltpu.make_async_copy(source(0, z), rows_buf, own_sem.at[0]),
        pltpu.make_async_copy(source(1, z), cols_buf, own_sem.at[1]),
        pltpu.make_async_copy(tokens, tok_buf, own_sem.at[2]),
    ]
    for copy in loads:
        copy.start()
    for copy in loads:
        copy.wait()
    stores = [
        pltpu.make_async_copy(rows_buf, slot(0, s, z), own_sem.at[3]),
        pltpu.make_async_copy(cols_buf, slot(1, s, z), own_sem.at[4]),
        pltpu.make_async_copy(tok_buf, pooled.at[pl.ds(pl.multiple_of(z * tok, tok), tok), :], own_sem.at[5]),
    ]
    for copy in stores:
        copy.start()

    passed = []
    for d in range(1, z_count):
        share(d)
        parts[d].wait_recv()
        owner = (z - d + z_count) % z_count
        for e in range(1, tp_count):
            copy = remote(part_of(owner, t), part_of(owner, t), tok_send.at[d, e], tok_recv.at[d, e],
                          tp=(t + e) % tp_count)
            copy.start()
            passed.append(copy)
        corner(d - 1)
    corner(z_count - 1)

    for copy in stores:
        copy.wait()
    for copy in passed:
        copy.wait()
    for d in range(1, z_count):
        parts[d].wait_send()
        for m in range(2):
            hops[m, d].wait_send()
    for (m, d, kind), copy in sides.items():
        if kind != d % 2:
            copy.wait_recv()
        copy.wait_send()


def spread_weights(frozen, base_out, tokens):
    z_count, s_count, tp_count = (lax.axis_size(n) for n in ("z", "s", "tp"))
    rows, units = frozen.shape[0], frozen.shape[1] // z_count
    tok, wide = tokens.shape
    width = rows * z_count * s_count
    dma = pltpu.SemaphoreType.DMA
    return pl.pallas_call(
        spread_kernel,
        out_shape=(
            jax.ShapeDtypeStruct((width, units), BF16),
            jax.ShapeDtypeStruct((units, width), BF16),
            jax.ShapeDtypeStruct((z_count * tok, wide), BF16),
        ),
        in_specs=[pl.BlockSpec(memory_space=pl.ANY)] * 3,
        out_specs=(pl.BlockSpec(memory_space=pl.ANY),) * 3,
        scratch_shapes=[
            pltpu.VMEM((rows, units), BF16),
            pltpu.VMEM((units, rows), BF16),
            pltpu.VMEM((tok, wide), BF16),
            dma((2, z_count)),
            dma((2, z_count)),
            dma((2, z_count, 3)),
            dma((2, z_count, 3)),
            dma((z_count, tp_count)),
            dma((z_count, tp_count)),
            dma((z_count,)),
            dma((z_count,)),
            dma((6,)),
        ],
        compiler_params=pltpu.CompilerParams(collective_id=0, has_side_effects=True),
    )(frozen, base_out, tokens)


def exchange_kernel(up, down, ups, downs, z_send, z_recv, s_send, s_recv, down_send, down_recv):
    z_count, s_count = lax.axis_size("z"), lax.axis_size("s")
    rep_count = z_count * s_count
    z, s = lax.axis_index("z"), lax.axis_index("s")
    me = z * s_count + s

    def remote(src, dst, send, recv, where):
        return pltpu.make_async_remote_copy(
            src_ref=src, dst_ref=dst, send_sem=send, recv_sem=recv, device_id=where, device_id_type=MESH
        )

    barrier = pltpu.get_barrier_semaphore()
    for k in range(1, rep_count):
        peer = (me + k) % rep_count
        where = {"z": peer // s_count, "s": peer % s_count}
        pl.semaphore_signal(barrier, inc=1, device_id=where, device_id_type=MESH)
    pl.semaphore_wait(barrier, rep_count - 1)

    hops, others = {}, []
    for d in range(1, z_count):
        hops[d] = remote(up, ups.at[me], z_send.at[d], z_recv.at[d], {"z": (z + d) % z_count})
        hops[d].start()

    def share(d, src):
        owner = ((z - d + z_count) % z_count) * s_count + s
        for e in range(1, s_count):
            copy = remote(src, ups.at[owner], s_send.at[d, e], s_recv.at[d, e], {"s": (s + e) % s_count})
            copy.start()
            others.append(copy)

    share(0, up)
    for k in range(1, rep_count):
        peer = (me + k) % rep_count
        where = {"z": peer // s_count, "s": peer % s_count}
        copy = remote(down.at[peer], downs.at[me], down_send.at[k], down_recv.at[k], where)
        copy.start()
        others.append(copy)
    ups[me] = up[...]
    downs[me] = down[me]
    for d in range(1, z_count):
        hops[d].wait_recv()
        share(d, ups.at[((z - d + z_count) % z_count) * s_count + s])
    for copy in others:
        copy.wait()
    for d in range(1, z_count):
        hops[d].wait_send()


def exchange(up, down):
    z_count, s_count = lax.axis_size("z"), lax.axis_size("s")
    rep_count = z_count * s_count
    dma = pltpu.SemaphoreType.DMA
    return pl.pallas_call(
        exchange_kernel,
        out_shape=(jax.ShapeDtypeStruct((rep_count,) + up.shape, BF16), jax.ShapeDtypeStruct(down.shape, BF16)),
        in_specs=[pl.BlockSpec(memory_space=pltpu.VMEM)] * 2,
        out_specs=(pl.BlockSpec(memory_space=pltpu.VMEM),) * 2,
        scratch_shapes=[
            dma((z_count,)),
            dma((z_count,)),
            dma((z_count, s_count)),
            dma((z_count, s_count)),
            dma((rep_count,)),
            dma((rep_count,)),
        ],
        compiler_params=pltpu.CompilerParams(collective_id=1, has_side_effects=True),
    )(up, down)


def shards(tokens, targets, frozen, base_out, factor_down, factor_up):
    z_count, s_count, tp_count = (lax.axis_size(n) for n in ("z", "s", "tp"))
    rep_count = z_count * s_count
    tok, width = tokens.shape
    ff = base_out.shape[0] * tp_count
    rank = factor_down.shape[1]
    a, b = factor_down[0], factor_up[0]
    step_scale = adapter_scale * width ** (-0.5)

    def permuted(x):
        blocks = x.reshape(x.shape[0], z_count, s_count, width // rep_count)
        return blocks.transpose(0, 2, 1, 3).reshape(x.shape)

    projected = jnp.einsum("td,rd->tr", tokens, a, preferred_element_type=F32).astype(BF16)
    padded = jnp.pad(projected, ((0, 0), (0, -rank % 128)))
    first, second, pooled = spread_weights(frozen, base_out, jnp.concatenate([permuted(tokens), padded], axis=1))
    group_tokens = pooled[:, :width]
    group_proj = pooled[:, width : width + rank].reshape(z_count, tok, rank)
    group_b = lax.all_to_all(b, "z", split_axis=1, concat_axis=0, tiled=True)
    units = group_b.shape[1]
    group_b = group_b.reshape(z_count, rank, units)

    lead = jnp.dot(group_tokens, first, preferred_element_type=F32)
    low = jnp.einsum("gtr,grf->gtf", group_proj, group_b, preferred_element_type=F32)
    preact = (lead + adapter_scale * low.reshape(lead.shape)) * width ** (-0.5)
    hidden = jnp.maximum(preact, 0.0).astype(BF16)
    part = jnp.dot(hidden, second, preferred_element_type=F32) * ff ** (-0.5)
    output = lax.psum_scatter(part.astype(BF16), ("z", "tp"), scatter_dimension=0, tiled=True)
    own = tok // tp_count
    wanted = lax.dynamic_slice_in_dim(targets, lax.axis_index("tp") * own, own, 0)
    out_grad = ((output.astype(F32) - permuted(wanted).astype(F32)) / tok).astype(BF16)
    group_grad = lax.all_gather(out_grad, ("z", "tp"), axis=0, tiled=True)
    hid_full = jnp.einsum("td,fd->tf", group_grad, second, preferred_element_type=F32)
    hid_grad = jnp.where(preact > 0, hid_full * ff ** (-0.5), 0.0).astype(BF16)
    hid_grad = hid_grad.reshape(z_count, tok, units)

    up_grad = step_scale * jnp.einsum("gtr,gtf->grf", group_proj, hid_grad, preferred_element_type=F32)
    back = jnp.einsum("grf,gtf->grt", group_b, hid_grad, preferred_element_type=F32)
    grads = lax.all_to_all(jnp.concatenate([up_grad, back], axis=2), "z", split_axis=0, concat_axis=0, tiled=True)
    up_grad = grads[:, :, :units].transpose(1, 0, 2).reshape(rank, z_count * units)
    back = lax.psum(jnp.sum(grads[:, :, units:], axis=0), "tp")
    high = lax.reduce_precision(back, 8, 7)
    middle = lax.reduce_precision(back - high, 8, 7)
    pieces = jnp.concatenate([high, middle, back - high - middle], axis=0).astype(BF16)
    products = jnp.dot(pieces, tokens, preferred_element_type=F32).reshape(3, rank, width)
    down_grad = step_scale * (products[0] + (products[1] + products[2]))

    new_a = a.astype(F32) - rate_down * down_grad
    new_b = b.astype(F32) - rate_up * up_grad
    rows = frozen.shape[0]
    wire = new_a.astype(BF16).reshape(rank, rep_count, rows).transpose(1, 0, 2)
    ups, downs = exchange(new_b.astype(BF16), wire)
    ups = ups.reshape(rep_count * rank, ups.shape[2])
    downs = downs.reshape(rep_count * rank, rows)
    delta = jnp.einsum("kd,kf->df", downs, ups, preferred_element_type=F32)
    merged = frozen.astype(F32) + adapter_scale / rep_count * delta
    return merged, new_a[None], new_b[None]


def solution(mesh):
    reps, tps = mesh.shape["rep"], mesh.shape["tp"]
    s_count = 1 << ((reps.bit_length() - 1) // 2)
    cut = Mesh(mesh.devices.reshape(reps // s_count, s_count, tps), ("z", "s", "tp"))
    in_specs = (
        P(REP, None),
        P(REP, None),
        P(REP, "tp"),
        P("tp", REP),
        P(REP, None, None),
        P(REP, None, "tp"),
    )
    out_specs = (P(REP, "tp"), P(REP, None, None), P(REP, None, "tp"))
    return jax.shard_map(shards, mesh=cut, in_specs=in_specs, out_specs=out_specs, check_vma=False)
```
